512 devices in a mesh: tp: 16 (over z_hi, y, core), dp: 32 (over z_lo, x).
Axes of the slice: x: 4, y: 4, z: 16 (z_hi: 2, z_lo: 8; z = z_hi * 8 + z_lo), core: 2. Of those that a mesh axis runs over, the one named last changes fastest.
Arguments:
- tokens: bfloat16 [2048, 4096], P(('tp', 'dp')), may hold values from -6 to 6
- norm_gain: float32 [4096], replicated, may hold values from 0.1 to 1.9
- gate_slots: bfloat16 [1536, 128, 128], P(('tp', 'dp')), may hold values from -0.1875 to 0.1875
- up_slots: bfloat16 [1536, 128, 128], P(('tp', 'dp')), may hold values from -0.1875 to 0.1875
- down_slots: bfloat16 [1536, 128, 128], P(('tp', 'dp')), may hold values from -0.09375 to 0.09375
- gate_ids: int32 [1536], P('tp'), may hold values from -1 to 223, as said below
- up_ids: int32 [1536], P('tp'), may hold values from -1 to 223, as said below
- down_ids: int32 [1536], P('tp'), may hold values from -1 to 223, as said below
Outputs:
- mixed: bfloat16 [2048, 4096], P(('tp', 'dp'))
The draws below stay inside these ranges and needn't reach their ends.
Inputs may be any that keep to these rules, and one draw needn't show every extreme that they name: `gate_ids`: each entry is -1 (an empty slot) or a block number j * 32 + k, j a hidden block of that tp index and k a block of the model width. The live numbers of one tp index are distinct and stand in its first slots; each tp index keeps at most 96 blocks, and one tp index keeps exactly 96. `up_ids`: as for gate_ids, drawn independently. `down_ids`: as for gate_ids, drawn independently.
All inputs are finite; a program needn't handle non-finite values.
Results may differ from the reference program's by a relative error of at most 0.015.
Values may be sent and summed in bfloat16 or wider, within the bound.
A program may use at most 128 MiB of HBM per device.

```python
import jax
import jax.numpy as jnp
from jax import lax

D = 4096
FF = 14336
BS = 128
TOKENS = 2048
CAP = 96
N_TP = 16


def block_list(key):
    hblocks = FF // (BS * N_TP)
    block_count = hblocks * (D // BS)
    count_key, busy_key, order_key, place_key = jax.random.split(key, 4)
    kept = jax.random.randint(count_key, (N_TP,), CAP // 6 + 1, CAP)
    busiest = jax.random.randint(busy_key, (), 0, N_TP)
    kept = jnp.where(jnp.arange(N_TP) == busiest, CAP, kept)
    shard_keys = jax.random.split(order_key, N_TP)
    shuffled = jax.vmap(lambda shard_key: jax.random.permutation(shard_key, block_count))(shard_keys)
    top_slot = jax.random.randint(place_key, (), 0, CAP)
    busy_row = shuffled[busiest]
    top_where = jnp.argmax(busy_row == block_count - 1)
    moved = busy_row[top_slot]
    busy_row = busy_row.at[top_where].set(moved).at[top_slot].set(block_count - 1)
    shuffled = shuffled.at[busiest].set(busy_row)
    slot_index = jnp.arange(CAP)
    listing = jnp.where(slot_index[None, :] < kept[:, None], shuffled[:, :CAP], -1)
    return listing.reshape(N_TP * CAP).astype(jnp.int32)


def draw_gate_ids(key, part):
    return block_list(jax.random.fold_in(key, 11))


def draw_up_ids(key, part):
    return block_list(jax.random.fold_in(key, 12))


def draw_down_ids(key, part):
    return block_list(jax.random.fold_in(key, 13))


def level_of(rng, dims, pieces, least, top_value):
    level = 1.0
    for dim, shards_of in pieces:
        steps = jax.random.uniform(jax.random.fold_in(jax.random.fold_in(rng, 6), dim), (shards_of,), jnp.float32, least / len(pieces), top_value / len(pieces))
        level = level * jnp.repeat(jnp.exp(steps), dims[dim] // shards_of).reshape((-1,) + (1,) * (len(dims) - 1 - dim))
    return level


def gaussian(stream_key, dims, scale, most, cuts=(), held_as=jnp.bfloat16):
    loudness = level_of(stream_key, dims, cuts, -0.22, 0.18) if cuts else 1.0
    array = jax.random.normal(stream_key, dims, jnp.float32) * scale * loudness
    return jnp.minimum(jnp.maximum(array, -most), most).astype(held_as)


def setup_inputs(seed: int = 0) -> dict:
    key_of = jax.random.split(jax.random.key(seed), 9)
    tokens = gaussian(key_of[0], (TOKENS, D), 1.0, 6.0, ((0, 512),))
    norm_gain = jnp.clip(1.0 + 0.18 * jax.random.normal(key_of[1], (D,), jnp.float32), 0.1, 1.9)
    gate_slots = gaussian(key_of[2], (N_TP * CAP, BS, BS), (D // 4) ** -0.5, 0.1875, ((0, 512),))
    up_slots = gaussian(key_of[3], (N_TP * CAP, BS, BS), (D // 4) ** -0.5, 0.1875, ((0, 512),))
    down_slots = gaussian(key_of[4], (N_TP * CAP, BS, BS), (FF // 4) ** -0.5, 0.09375, ((0, 512),))
    gate_ids = draw_gate_ids(jax.random.fold_in(key_of[8], 71), 0)
    up_ids = draw_up_ids(jax.random.fold_in(key_of[8], 71), 0)
    down_ids = draw_down_ids(jax.random.fold_in(key_of[8], 71), 0)
    return dict(tokens=tokens, norm_gain=norm_gain, gate_slots=gate_slots, up_slots=up_slots, down_slots=down_slots, gate_ids=gate_ids, up_ids=up_ids, down_ids=down_ids)


EPSILON = 1e-05

def normalize(tokens, norm_gain):
    values = tokens.astype(jnp.float32)
    meansq = lax.optimization_barrier(jnp.mean(values * values, axis=-1, keepdims=True))
    return (values * lax.rsqrt(meansq + EPSILON) * norm_gain).astype(jnp.bfloat16)

def shard_blocks(slot_values, slot_ids, hblocks, kblocks):
    block_count = hblocks * kblocks
    flat_index = jnp.where(slot_ids >= 0, slot_ids, block_count).astype(jnp.int32)
    block_grid = jnp.zeros((block_count + 1, BS, BS), slot_values.dtype).at[flat_index].set(slot_values)
    return block_grid[:block_count].reshape(hblocks, kblocks, BS, BS)

def reference(tokens, norm_gain, gate_slots, up_slots, down_slots, gate_ids, up_ids, down_ids):
    hblocks = FF // (BS * N_TP)
    kblocks = D // BS
    normed = normalize(tokens, norm_gain)

    def one_shard(running, shard):
        gate_vals, up_vals, down_vals, gate_list, up_list, down_list = shard
        gate_weight = shard_blocks(gate_vals, gate_list, hblocks, kblocks).transpose(1, 2, 0, 3).reshape(D, hblocks * BS)
        up_weight = shard_blocks(up_vals, up_list, hblocks, kblocks).transpose(1, 2, 0, 3).reshape(D, hblocks * BS)
        down_weight = shard_blocks(down_vals, down_list, hblocks, kblocks).transpose(0, 2, 1, 3).reshape(hblocks * BS, D)
        gate_act = jnp.dot(normed, gate_weight, preferred_element_type=jnp.float32)
        up_act = jnp.dot(normed, up_weight, preferred_element_type=jnp.float32)
        hidden = (jax.nn.silu(gate_act) * up_act).astype(jnp.bfloat16)
        contribution = jnp.dot(hidden, down_weight, preferred_element_type=jnp.float32).astype(jnp.bfloat16)
        contribution = lax.optimization_barrier(contribution)
        return (running + contribution.astype(jnp.float32), None)
    stacked = (gate_slots.reshape(N_TP, CAP, BS, BS), up_slots.reshape(N_TP, CAP, BS, BS), down_slots.reshape(N_TP, CAP, BS, BS), gate_ids.reshape(N_TP, CAP), up_ids.reshape(N_TP, CAP), down_ids.reshape(N_TP, CAP))
    branch_sum, unused = lax.scan(one_shard, jnp.zeros((TOKENS, D), jnp.float32), stacked)
    return (tokens.astype(jnp.float32) + branch_sum).astype(jnp.bfloat16)
```

```python
import jax
import jax.numpy as jnp
from jax import lax
from jax.experimental import pallas as pl
from jax.experimental.pallas import tpu as pltpu
from jax.sharding import PartitionSpec as P

EPSILON = 1e-05
MESH = pl.DeviceIdType.MESH
BS = 128
CAP = 96
D = 4096
CH = 4
CW = D // CH


def layer(tok_ref, gain_ref, tab_ref, g_hbm, u_hbm, d_hbm, out_ref,
          wg, wu, wd, tabs, tab_s, xz, xf, xa, gate_s, hid_s, sb, rb, sf, gb, rg,
          own, swap, zr, zs, xr, xs, fr, fs, cr, cs, tsem, ssem, gr, gs, yr, ys, yr2, ys2, gr2, gs2):
    t = lax.axis_index("tp")
    d = lax.axis_index("dp")
    hi, y, c = t // 8, (t // 2) % 4, t % 2
    zl, x = d // 4, d % 4
    half, ze = zl // 4, zl % 4
    g = hi * 2 + half

    def dev(hi=hi, y=y, c=c, half=half, ze=ze, x=x):
        return {"tp": hi * 8 + y * 2 + c, "dp": (half * 4 + ze) * 4 + x}

    partner = dev(c=1 - c, half=1 - half)
    zpeer = [None] + [dev(ze=(ze + i) % 4) for i in (1, 2, 3)]
    right, left = dev(x=(x + 1) % 4), dev(x=(x + 3) % 4)
    sib = dev(c=1 - c)
    ypeer = [None] + [dev(y=(y + i) % 4) for i in (1, 2, 3)]
    gpeer = [None]
    for i in (1, 2, 3):
        o = (g + i) % 4
        gpeer.append(dev(hi=o // 2, half=o % 2))

    barrier = pltpu.get_barrier_semaphore()
    peers = [partner, right, left, sib] + zpeer[1:] + ypeer[1:] + gpeer[1:]
    for p in peers:
        pl.semaphore_signal(barrier, inc=1, device_id=p, device_id_type=MESH)
    pl.semaphore_wait(barrier, len(peers))

    W = (wg, wu, wd)
    src = (g_hbm, u_hbm, d_hbm)
    is_home = c == half
    pending = []

    def remote(a, b, s, r, p):
        return pltpu.make_async_remote_copy(
            src_ref=a, dst_ref=b, send_sem=s, recv_sem=r, device_id=p, device_id_type=MESH)

    def piece(q, n, xx):
        p = 16 * c + 4 * ((ze + 4 - n) % 4) + xx % 4
        return W[q].at[pl.ds(p * 3, 3)]

    def swap_copy(q):
        p = 16 * half + 4 * ze + x
        return remote(src[q], W[q].at[pl.ds(p * 3, 3)], swap.at[q], own.at[q], partner)

    def home_copy(q):
        return pltpu.make_async_copy(src[q], piece(q, 0, x), own.at[q])

    @pl.when(is_home)
    def _():
        for q in range(3):
            home_copy(q).start()

    @pl.when(jnp.logical_not(is_home))
    def _():
        for q in range(3):
            swap_copy(q).start()

    tcopy = remote(tab_ref, tabs.at[c], ssem.at[0], tsem.at[0], sib)
    tcopy.start()
    tabs[2] = tab_ref[...]

    v = tok_ref[...].astype(jnp.float32)
    ms = jnp.mean(v * v, axis=-1, keepdims=True)
    xz[g] = (v * lax.rsqrt(ms + EPSILON) * gain_ref[...]).astype(jnp.bfloat16)
    gcopies = [remote(xz.at[g], xz.at[g], gs.at[i], gr.at[i], gpeer[i]) for i in (1, 2, 3)]
    for cp in gcopies:
        cp.start()
    pending.extend(gcopies)

    for q in range(3):
        W[q][CAP] = jnp.zeros((BS, BS), jnp.bfloat16)

    def core_send(q, ref):
        remote(ref, ref, cs.at[q], cr.at[q], sib).start()

    def x_send(q, n):
        ref = piece(q, n, x)
        for k, p in ((0, right), (1, left)):
            cp = remote(ref, ref, xs.at[q, k, n], xr.at[q, k, n], p)
            cp.start()
            pending.append(cp)

    def first(q):
        home_copy(q).wait()
        ref = piece(q, 0, x)
        for i in (2, 1, 3):
            cp = remote(ref, ref, zs.at[q, i], zr.at[q, i], zpeer[i])
            cp.start()
            pending.append(cp)
        x_send(q, 0)
        core_send(q, ref)

    def stage1(q):
        for n in (1, 3, 2):
            ref = piece(q, n, x)
            remote(ref, ref, zs.at[q, n], zr.at[q, n], zpeer[n]).wait_recv()
            x_send(q, n)
            core_send(q, ref)

    def stage2(q):
        for n in (0, 1, 3, 2):
            fl, fright = piece(q, n, x + 3), piece(q, n, x + 1)
            remote(fl, fl, xs.at[q, 0, n], xr.at[q, 0, n], right).wait_recv()
            remote(fright, fright, xs.at[q, 1, n], xr.at[q, 1, n], left).wait_recv()
            ref, p = (fl, right) if n < 2 else (fright, left)
            cp = remote(ref, ref, fs.at[q, n], fr.at[q, n], p)
            cp.start()
            pending.append(cp)
            core_send(q, fl)
            core_send(q, fright)

    def stage3(q):
        for n in (0, 1, 3, 2):
            ref = piece(q, n, x + 2)
            remote(ref, ref, fs.at[q, n], fr.at[q, n], right).wait_recv()
            core_send(q, ref)

    def stage4(q):
        ref = W[q].at[pl.ds(48 * (1 - c), 48)]
        remote(ref, ref, cs.at[q], cr.at[q], sib).wait_recv()

    def w4(q, j, k):
        def one(jj, kk):
            b = jj * 32 + kk
            return W[q][tab_s[2 * q + b // 128, b % 128]]
        return one(j, k), one(j, k + 1), one(j + 1, k), one(j + 1, k + 1)

    def project(q, jp):
        acc = jnp.zeros((64, 256), jnp.float32)
        for kk in range(16):
            a, b, e, f = w4(q, 2 * jp, 2 * kk)
            w = jnp.concatenate(
                [jnp.concatenate([a, e], axis=1), jnp.concatenate([b, f], axis=1)], axis=0)
            xx = xa[:, :, 256 * kk:256 * kk + 256].reshape(64, 256)
            acc = acc + jnp.dot(xx, w, preferred_element_type=jnp.float32)
        return acc

    first(0)
    for i in (1, 2, 3):
        remote(xz.at[(g + 4 - i) % 4], xz.at[(g + 4 - i) % 4], gs.at[i], gr.at[i], gpeer[i]).wait_recv()
    for i in range(4):
        xf[4 * i:4 * i + 4, :] = xz[i].astype(jnp.float32)
    xa[y] = xf[...].astype(jnp.bfloat16)
    ycopies = [remote(xa.at[y], xa.at[y], ys.at[i], yr.at[i], ypeer[i]) for i in (1, 2, 3)]
    for cp in ycopies:
        cp.start()
    pending.extend(ycopies)
    first(1)
    first(2)

    remote(tab_ref, tabs.at[1 - c], ssem.at[0], tsem.at[0], sib).wait_recv()
    mine = pltpu.make_async_copy(tabs.at[jnp.where(is_home, 2, half)], tab_s, tsem.at[1])
    mine.start()
    mine.wait()

    stage1(0)
    stage2(0)
    stage1(1)
    stage3(0)
    stage2(1)
    for i in (1, 2, 3):
        ref = xa.at[(y + 4 - i) % 4]
        remote(ref, ref, ys.at[i], yr.at[i], ypeer[i]).wait_recv()
    stage4(0)

    @pl.loop(0, 4)
    def _(jp):
        gate_s[jp] = project(0, jp)

    stage1(2)
    stage3(1)
    stage2(2)
    stage4(1)

    @pl.loop(0, 4)
    def _(jp):
        up = project(1, jp)
        ga = gate_s[jp]
        hid_s[jp] = (ga / (1.0 + jnp.exp(-ga)) * up).astype(jnp.bfloat16)

    stage3(2)
    stage4(2)

    def y_copy(n, i):
        return remote(sb.at[n, (y + i) % 4], rb.at[n, i], ys2.at[n, i], yr2.at[n, i], ypeer[i])

    def g_copy(n, i):
        return remote(gb.at[n, (g + i) % 4], rg.at[n, i], gs2.at[n, i], gr2.at[n, i], gpeer[i])

    @pl.loop(0, CH)
    def _(n):
        for kp in range(4):
            acc = jnp.zeros((64, 256), jnp.float32)
            for jp in range(4):
                k = n * 8 + 2 * kp
                a, e, b, f = w4(2, 2 * jp, k)
                w = jnp.concatenate(
                    [jnp.concatenate([a, e], axis=1), jnp.concatenate([b, f], axis=1)], axis=0)
                acc = acc + jnp.dot(hid_s[jp], w, preferred_element_type=jnp.float32)
            sb[n, :, :, 256 * kp:256 * kp + 256] = acc.astype(jnp.bfloat16).reshape(4, 16, 256)
        for i in (1, 2, 3):
            y_copy(n, i).start()

    @pl.loop(0, CH)
    def _(n):
        for i in (1, 2, 3):
            y_copy(n, i).wait_recv()
        s = sb[n, y].astype(jnp.float32)
        for i in (1, 2, 3):
            s = s + rb[n, i].astype(jnp.float32)
        sf[...] = s
        for i in range(4):
            gb[n, i] = sf[4 * i:4 * i + 4, :].astype(jnp.bfloat16)
        for i in (1, 2, 3):
            g_copy(n, i).start()

    for n in range(CH):
        for i in (1, 2, 3):
            g_copy(n, i).wait_recv()
        s = gb[n, g].astype(jnp.float32)
        for i in (1, 2, 3):
            s = s + rg[n, i].astype(jnp.float32)
        cols = slice(n * CW, (n + 1) * CW)
        out_ref[:, cols] = (tok_ref[:, cols].astype(jnp.float32) + s).astype(jnp.bfloat16)

    for cp in pending:
        cp.wait_send()
    tcopy.wait_send()
    for q in range(3):
        ref = W[q].at[pl.ds(48 * c, 48)]
        remote(ref, ref, cs.at[q], cr.at[q], sib).wait_send()
    for n in range(CH):
        for i in (1, 2, 3):
            y_copy(n, i).wait_send()
            g_copy(n, i).wait_send()

    @pl.when(jnp.logical_not(is_home))
    def _():
        for q in range(3):
            swap_copy(q).wait_send()


def shards(tokens, norm_gain, gate_slots, up_slots, down_slots, gate_ids, up_ids, down_ids):
    ids = jnp.stack([gate_ids, up_ids, down_ids])
    hit = ids[:, None, :] == jnp.arange(256, dtype=jnp.int32)[None, :, None]
    tab = jnp.min(jnp.where(hit, jnp.arange(CAP, dtype=jnp.int32), CAP), axis=-1)
    tab = jnp.pad(tab.reshape(6, 128), ((0, 2), (0, 0)))
    bf, f32 = jnp.bfloat16, jnp.float32
    dma = pltpu.SemaphoreType.DMA
    vm = pl.BlockSpec(memory_space=pltpu.VMEM)
    hbm = pl.BlockSpec(memory_space=pl.ANY)
    return pl.pallas_call(
        layer,
        out_shape=jax.ShapeDtypeStruct((4, D), bf),
        in_specs=[vm, vm, vm, hbm, hbm, hbm],
        out_specs=vm,
        scratch_shapes=[
            pltpu.VMEM((CAP + 1, BS, BS), bf),
            pltpu.VMEM((CAP + 1, BS, BS), bf),
            pltpu.VMEM((CAP + 1, BS, BS), bf),
            pltpu.VMEM((3, 8, 128), jnp.int32),
            pltpu.SMEM((8, 128), jnp.int32),
            pltpu.VMEM((4, 4, D), bf),
            pltpu.VMEM((16, D), f32),
            pltpu.VMEM((4, 16, D), bf),
            pltpu.VMEM((4, 64, 256), f32),
            pltpu.VMEM((4, 64, 256), bf),
            pltpu.VMEM((CH, 4, 16, CW), bf),
            pltpu.VMEM((CH, 4, 16, CW), bf),
            pltpu.VMEM((16, CW), f32),
            pltpu.VMEM((CH, 4, 4, CW), bf),
            pltpu.VMEM((CH, 4, 4, CW), bf),
            dma((3,)), dma((3,)), dma((3, 4)), dma((3, 4)), dma((3, 2, 4)), dma((3, 2, 4)),
            dma((3, 4)), dma((3, 4)), dma((3,)), dma((3,)), dma((2,)), dma((1,)),
            dma((4,)), dma((4,)), dma((4,)), dma((4,)),
            dma((CH, 4)), dma((CH, 4)), dma((CH, 4)), dma((CH, 4)),
        ],
        compiler_params=pltpu.CompilerParams(
            collective_id=0, has_side_effects=True, vmem_limit_bytes=40 << 20),
    )(tokens, norm_gain.reshape(1, D), tab, gate_slots, up_slots, down_slots)


def solution(mesh):
    placed = (
        P(("tp", "dp"), None),
        P(),
        P(("tp", "dp"), None, None),
        P(("tp", "dp"), None, None),
        P(("tp", "dp"), None, None),
        P("tp"),
        P("tp"),
        P("tp"),
    )
    return jax.shard_map(
        shards, mesh=mesh, in_specs=placed, out_specs=P(("tp", "dp"), None), check_vma=False
    )
```

```python
import jax
import jax.numpy as jnp
from jax import lax
from jax.experimental import pallas as pl
from jax.experimental.pallas import tpu as pltpu
from jax.sharding import PartitionSpec as P

EPSILON = 1e-05
MESH = pl.DeviceIdType.MESH
BS = 128
CAP = 96
D = 4096
CH = 4
CW = D // CH


def layer(tok_ref, gain_ref, tab_ref, g_hbm, u_hbm, d_hbm, out_ref,
          wg, wu, wd, tabs, tab_s, xz, xf, xa, gate_s, hid_s, sb, rb, sf, gb, rg,
          swap, zr, zs, xr, xs, fr, fs, cr, cs, tsem, ssem, gr, gs, yr, ys, yr2, ys2, gr2, gs2):
    t = lax.axis_index("tp")
    d = lax.axis_index("dp")
    hi, y, c = t // 8, (t // 2) % 4, t % 2
    zl, x = d // 4, d % 4
    half, ze = zl // 4, zl % 4
    g = hi * 2 + half

    def dev(hi=hi, y=y, c=c, half=half, ze=ze, x=x):
        return {"tp": hi * 8 + y * 2 + c, "dp": (half * 4 + ze) * 4 + x}

    partner = dev(c=1 - c, half=1 - half)
    right, left = dev(x=(x + 1) % 4), dev(x=(x + 3) % 4)
    sib = dev(c=1 - c)
    ypeer = [None] + [dev(y=(y + i) % 4) for i in (1, 2, 3)]
    gpeer = [None]
    for i in (1, 2, 3):
        o = (g + i) % 4
        gpeer.append(dev(hi=o // 2, half=o % 2))

    barrier = pltpu.get_barrier_semaphore()
    peers = [partner, right, left, sib] + ypeer[1:] + gpeer[1:] + [
        dev(ze=(ze + 1) % 4), dev(ze=(ze + 3) % 4)]
    for p in peers:
        pl.semaphore_signal(barrier, inc=1, device_id=p, device_id_type=MESH)
    W = (wg, wu, wd)
    src = (g_hbm, u_hbm, d_hbm)
    is_home = c == half
    pending = []

    def remote(a, b, s, r, p):
        return pltpu.make_async_remote_copy(
            src_ref=a, dst_ref=b, send_sem=s, recv_sem=r, device_id=p, device_id_type=MESH)

    edge = (ze == 0) | (ze == 3)
    key = (0, jnp.where(ze == 0, 3, 1), jnp.where(edge, 2, 3),
           jnp.where(ze == 0, 1, jnp.where(ze == 3, 3, 2)))
    zpos = [(ze + 4 - k) % 4 for k in key]
    goes_up = [(ze < 3) & (ze >= k) for k in key]
    goes_down = [ze > 0] + [(ze > 0) & (ze < k) for k in key[1:]]
    above = dev(ze=jnp.minimum(ze + 1, 3))
    below = dev(ze=jnp.maximum(ze - 1, 0))

    def piece(q, m, xx):
        return W[q].at[pl.ds((16 * c + 4 * zpos[m] + xx % 4) * 3, 3)]

    def z_up(q, m):
        ref = piece(q, m, x)
        return remote(ref, ref, zs.at[q, 0, m], zr.at[q, (key[m] + 1) % 4], above)

    def z_down(q, m):
        ref = piece(q, m, x)
        return remote(ref, ref, zs.at[q, 1, m], zr.at[q, (key[m] + 3) % 4], below)

    def swap_copy(q):
        p = 16 * half + 4 * ze + x
        return remote(src[q], W[q].at[pl.ds(p * 3, 3)], swap.at[q], zr.at[q, 0], partner)

    def home_copy(q):
        return pltpu.make_async_copy(src[q], piece(q, 0, x), zr.at[q, 0])

    @pl.when(is_home)
    def _():
        for q in range(3):
            home_copy(q).start()

    v = tok_ref[...].astype(jnp.float32)
    ms = jnp.mean(v * v, axis=-1, keepdims=True)
    xz[g] = (v * lax.rsqrt(ms + EPSILON) * gain_ref[...]).astype(jnp.bfloat16)
    for q in range(3):
        W[q][CAP] = jnp.zeros((BS, BS), jnp.bfloat16)

    tabs[2] = tab_ref[...]
    pl.semaphore_wait(barrier, len(peers))

    gcopies = [remote(xz.at[g], xz.at[g], gs.at[i], gr.at[i], gpeer[i]) for i in (1, 2, 3)]
    pending.extend(gcopies)

    @pl.when(jnp.logical_not(is_home))
    def _():
        for q in range(3):
            swap_copy(q).start()

    tcopy = remote(tab_ref, tabs.at[c], ssem.at[0], tsem.at[0], sib)
    tcopy.start()

    def core_send(q, ref):
        remote(ref, ref, cs.at[q], cr.at[q], sib).start()

    def x_copy(q, k, m):
        ref = piece(q, m, x)
        return remote(ref, ref, xs.at[q, k, m], xr.at[q, k, m], left if k else right)

    def f_copy(q, m):
        ref, p = (piece(q, m, x + 1), left) if m % 2 else (piece(q, m, x + 3), right)
        return remote(ref, ref, fs.at[q, m], fr.at[q, m], p)

    def x_send(q, m):
        x_copy(q, 0, m).start()
        x_copy(q, 1, m).start()

    def step(q, m):
        ref = piece(q, m, x)
        remote(ref, ref, zs.at[q, 0, m], zr.at[q, key[m]], above).wait_recv()

        @pl.when(goes_up[m])
        def _():
            z_up(q, m).start()

        @pl.when(goes_down[m])
        def _():
            z_down(q, m).start()

        x_send(q, m)
        core_send(q, ref)

    def forward(q, m):
        fl, fright = piece(q, m, x + 3), piece(q, m, x + 1)
        remote(fl, fl, xs.at[q, 0, m], xr.at[q, 0, m], right).wait_recv()
        remote(fright, fright, xs.at[q, 1, m], xr.at[q, 1, m], left).wait_recv()
        f_copy(q, m).start()
        core_send(q, fl)
        core_send(q, fright)

    def far(q, m):
        ref = piece(q, m, x + 2)
        remote(ref, ref, fs.at[q, m], fr.at[q, m], right).wait_recv()
        core_send(q, ref)

    def stage4(q):
        ref = W[q].at[pl.ds(48 * (1 - c), 48)]
        remote(ref, ref, cs.at[q], cr.at[q], sib).wait_recv()

    def w4(q, j, k):
        def one(jj, kk):
            b = jj * 32 + kk
            return W[q][tab_s[2 * q + b // 128, b % 128]]
        return one(j, k), one(j, k + 1), one(j + 1, k), one(j + 1, k + 1)

    def project(q, jp):
        acc = jnp.zeros((64, 256), jnp.float32)
        for kk in range(16):
            a, b, e, f = w4(q, 2 * jp, 2 * kk)
            w = jnp.concatenate(
                [jnp.concatenate([a, e], axis=1), jnp.concatenate([b, f], axis=1)], axis=0)
            xx = xa[:, :, 256 * kk:256 * kk + 256].reshape(64, 256)
            acc = acc + jnp.dot(xx, w, preferred_element_type=jnp.float32)
        return acc

    def tokens_g():
        for i in (1, 2, 3):
            ref = xz.at[(g + 4 - i) % 4]
            remote(ref, ref, gs.at[i], gr.at[i], gpeer[i]).wait_recv()
        for i in range(4):
            xf[4 * i:4 * i + 4, :] = xz[i].astype(jnp.float32)
        xa[y] = xf[...].astype(jnp.bfloat16)
        for i in (1, 2, 3):
            cp = remote(xa.at[y], xa.at[y], ys.at[i], yr.at[i], ypeer[i])
            cp.start()
            pending.append(cp)

    def tokens_y():
        for i in (1, 2, 3):
            ref = xa.at[(y + 4 - i) % 4]
            remote(ref, ref, ys.at[i], yr.at[i], ypeer[i]).wait_recv()
        remote(tab_ref, tabs.at[1 - c], ssem.at[0], tsem.at[0], sib).wait_recv()
        mine = pltpu.make_async_copy(tabs.at[jnp.where(is_home, 2, half)], tab_s, tsem.at[1])
        mine.start()
        mine.wait()

    items = [(q, m) for q in range(3) for m in range(4)]

    @pl.when(is_home)
    def _():
        for q in range(3):
            step(q, 0)

    for p in range(12):
        q, m = items[p]
        if m == 0:
            @pl.when(jnp.logical_not(is_home))
            def _():
                step(q, 0)
        else:
            step(q, m)
        if p >= 4:
            forward(*items[p - 4])
        if p >= 8:
            far(*items[p - 8])
        if p == 6:
            for cp in gcopies:
                cp.start()
    forward(*items[8])
    tokens_g()
    forward(*items[9])
    forward(*items[10])
    forward(*items[11])
    for p in (4, 5):
        far(*items[p])
    tokens_y()
    stage4(0)

    @pl.loop(0, 4)
    def _(jp):
        gate_s[jp] = project(0, jp)

    for p in (6, 7, 8, 9):
        far(*items[p])
    stage4(1)

    @pl.loop(0, 4)
    def _(jp):
        up = project(1, jp)
        ga = gate_s[jp]
        hid_s[jp] = (ga / (1.0 + jnp.exp(-ga)) * up).astype(jnp.bfloat16)

    for p in (10, 11):
        far(*items[p])
    stage4(2)

    def y_copy(n, i):
        return remote(sb.at[n, (y + i) % 4], rb.at[n, i], ys2.at[n, i], yr2.at[n, i], ypeer[i])

    def g_copy(n, i):
        return remote(gb.at[n, (g + i) % 4], rg.at[n, i], gs2.at[n, i], gr2.at[n, i], gpeer[i])

    @pl.loop(0, CH)
    def _(n):
        for kp in range(4):
            acc = jnp.zeros((64, 256), jnp.float32)
            for jp in range(4):
                k = n * 8 + 2 * kp
                a, e, b, f = w4(2, 2 * jp, k)
                w = jnp.concatenate(
                    [jnp.concatenate([a, e], axis=1), jnp.concatenate([b, f], axis=1)], axis=0)
                acc = acc + jnp.dot(hid_s[jp], w, preferred_element_type=jnp.float32)
            sb[n, :, :, 256 * kp:256 * kp + 256] = acc.astype(jnp.bfloat16).reshape(4, 16, 256)
        for i in (1, 2, 3):
            y_copy(n, i).start()

    @pl.loop(0, CH)
    def _(n):
        for i in (1, 2, 3):
            y_copy(n, i).wait_recv()
        s = sb[n, y].astype(jnp.float32)
        for i in (1, 2, 3):
            s = s + rb[n, i].astype(jnp.float32)
        sf[...] = s
        for i in range(4):
            gb[n, i] = sf[4 * i:4 * i + 4, :].astype(jnp.bfloat16)
        for i in (1, 2, 3):
            g_copy(n, i).start()

    for n in range(CH):
        for i in (1, 2, 3):
            g_copy(n, i).wait_recv()
        s = gb[n, g].astype(jnp.float32)
        for i in (1, 2, 3):
            s = s + rg[n, i].astype(jnp.float32)
        cols = slice(n * CW, (n + 1) * CW)
        out_ref[:, cols] = (tok_ref[:, cols].astype(jnp.float32) + s).astype(jnp.bfloat16)

    for cp in pending:
        cp.wait_send()
    tcopy.wait_send()
    for q in range(3):
        for m in range(4):
            x_copy(q, 0, m).wait_send()
            x_copy(q, 1, m).wait_send()
            f_copy(q, m).wait_send()
        for m in range(4):
            @pl.when(goes_up[m])
            def _():
                z_up(q, m).wait_send()

            @pl.when(goes_down[m])
            def _():
                z_down(q, m).wait_send()

    for q in range(3):
        ref = W[q].at[pl.ds(48 * c, 48)]
        remote(ref, ref, cs.at[q], cr.at[q], sib).wait_send()
    for n in range(CH):
        for i in (1, 2, 3):
            y_copy(n, i).wait_send()
            g_copy(n, i).wait_send()

    @pl.when(jnp.logical_not(is_home))
    def _():
        for q in range(3):
            swap_copy(q).wait_send()


def shards(tokens, norm_gain, gate_slots, up_slots, down_slots, gate_ids, up_ids, down_ids):
    ids = jnp.stack([gate_ids, up_ids, down_ids])
    hit = ids[:, None, :] == jnp.arange(256, dtype=jnp.int32)[None, :, None]
    tab = jnp.min(jnp.where(hit, jnp.arange(CAP, dtype=jnp.int32), CAP), axis=-1)
    tab = jnp.pad(tab.reshape(6, 128), ((0, 2), (0, 0)))
    bf, f32 = jnp.bfloat16, jnp.float32
    dma = pltpu.SemaphoreType.DMA
    vm = pl.BlockSpec(memory_space=pltpu.VMEM)
    hbm = pl.BlockSpec(memory_space=pltpu.MemorySpace.HBM)
    return pl.pallas_call(
        layer,
        out_shape=jax.ShapeDtypeStruct((4, D), bf),
        in_specs=[vm, vm, vm, hbm, hbm, hbm],
        out_specs=vm,
        scratch_shapes=[
            pltpu.VMEM((CAP + 1, BS, BS), bf),
            pltpu.VMEM((CAP + 1, BS, BS), bf),
            pltpu.VMEM((CAP + 1, BS, BS), bf),
            pltpu.VMEM((3, 8, 128), jnp.int32),
            pltpu.SMEM((8, 128), jnp.int32),
            pltpu.VMEM((4, 4, D), bf),
            pltpu.VMEM((16, D), f32),
            pltpu.VMEM((4, 16, D), bf),
            pltpu.VMEM((4, 64, 256), f32),
            pltpu.VMEM((4, 64, 256), bf),
            pltpu.VMEM((CH, 4, 16, CW), bf),
            pltpu.VMEM((CH, 4, 16, CW), bf),
            pltpu.VMEM((16, CW), f32),
            pltpu.VMEM((CH, 4, 4, CW), bf),
            pltpu.VMEM((CH, 4, 4, CW), bf),
            dma((3,)), dma((3, 4)), dma((3, 2, 4)), dma((3, 2, 4)), dma((3, 2, 4)),
            dma((3, 4)), dma((3, 4)), dma((3,)), dma((3,)), dma((2,)), dma((1,)),
            dma((4,)), dma((4,)), dma((4,)), dma((4,)),
            dma((CH, 4)), dma((CH, 4)), dma((CH, 4)), dma((CH, 4)),
        ],
        compiler_params=pltpu.CompilerParams(
            collective_id=0, has_side_effects=True, vmem_limit_bytes=63 << 20),
    )(tokens, norm_gain.reshape(1, D), tab, gate_slots, up_slots, down_slots)


def solution(mesh):
    placed = (
        P(("tp", "dp"), None),
        P(),
        P(("tp", "dp"), None, None),
        P(("tp", "dp"), None, None),
        P(("tp", "dp"), None, None),
        P("tp"),
        P("tp"),
        P("tp"),
    )
    return jax.shard_map(
        shards, mesh=mesh, in_specs=placed, out_specs=P(("tp", "dp"), None), check_vma=False
    )
```

```python
import jax
import jax.numpy as jnp
from jax import lax
from jax.experimental import pallas as pl
from jax.experimental.pallas import tpu as pltpu
from jax.sharding import PartitionSpec as P

EPSILON = 1e-05
MESH = pl.DeviceIdType.MESH
BS = 128
CAP = 96
D = 4096
CH = 4
CW = D // CH


def layer(tok_ref, gain_ref, tab_ref, g_hbm, u_hbm, d_hbm, out_ref,
          wg, wu, wd, tabs, tab_s, xz, xf, xa, gate_s, hid_s, sb, rb, sf, gb, rg, stage,
          swap, staged, zr, zs, xr, xs, fr, fs, cr, cs, tsem, ssem, gr, gs, yr, ys, yr2, ys2, gr2, gs2):
    t = lax.axis_index("tp")
    d = lax.axis_index("dp")
    hi, y, c = t // 8, (t // 2) % 4, t % 2
    zl, x = d // 4, d % 4
    half, ze = zl // 4, zl % 4
    g = hi * 2 + half

    def dev(hi=hi, y=y, c=c, half=half, ze=ze, x=x):
        return {"tp": hi * 8 + y * 2 + c, "dp": (half * 4 + ze) * 4 + x}

    entry = dev(c=1 - c, half=1 - half, ze=3 * half)
    across = [dev(c=1 - c, half=1 - half, ze=i) for i in range(4)]
    right, left = dev(x=(x + 1) % 4), dev(x=(x + 3) % 4)
    sib = dev(c=1 - c)
    ypeer = [None] + [dev(y=(y + i) % 4) for i in (1, 2, 3)]
    gpeer = [None]
    for i in (1, 2, 3):
        o = (g + i) % 4
        gpeer.append(dev(hi=o // 2, half=o % 2))

    barrier = pltpu.get_barrier_semaphore()
    peers = across + [right, left, sib] + ypeer[1:] + gpeer[1:] + [
        dev(ze=(ze + 1) % 4), dev(ze=(ze + 3) % 4)]
    for p in peers:
        pl.semaphore_signal(barrier, inc=1, device_id=p, device_id_type=MESH)
    W = (wg, wu, wd)
    src = (g_hbm, u_hbm, d_hbm)
    is_home = c == half
    pending = []

    def remote(a, b, s, r, p):
        return pltpu.make_async_remote_copy(
            src_ref=a, dst_ref=b, send_sem=s, recv_sem=r, device_id=p, device_id_type=MESH)

    edge = (ze == 0) | (ze == 3)
    order = (0, jnp.where(ze == 0, 3, 1), jnp.where(edge, 2, 3),
             jnp.where(ze == 0, 1, jnp.where(ze == 3, 3, 2)))
    zpos = [jnp.where(is_home, (ze + 4 - order[m]) % 4, jnp.where(half == 0, m, 3 - m)) for m in range(4)]
    key = [jnp.where(is_home, order[m], m) for m in range(4)]
    goes_up = [(ze < 3) & jnp.where(is_home, ze >= order[m], half == 1) for m in range(4)]
    goes_down = [(ze > 0) & jnp.where(is_home, (ze < order[m]) | (m == 0), half == 0) for m in range(4)]
    above = dev(ze=jnp.minimum(ze + 1, 3))
    below = dev(ze=jnp.maximum(ze - 1, 0))

    def piece(q, m, xx):
        return W[q].at[pl.ds((16 * c + 4 * zpos[m] + xx % 4) * 3, 3)]

    def z_up(q, m):
        ref = piece(q, m, x)
        return remote(ref, ref, zs.at[q, 0, m], zr.at[q, jnp.where(is_home, (order[m] + 1) % 4, m)], above)

    def z_down(q, m):
        ref = piece(q, m, x)
        return remote(ref, ref, zs.at[q, 1, m], zr.at[q, jnp.where(is_home, (order[m] + 3) % 4, m)], below)

    def swap_copy(q):
        p = 16 * half + 4 * ze + x
        m = jnp.where(half == 1, ze, 3 - ze)
        return remote(stage.at[q], W[q].at[pl.ds(p * 3, 3)], swap.at[q], zr.at[q, m], entry)

    def home_copy(q):
        return pltpu.make_async_copy(src[q], piece(q, 0, x), zr.at[q, 0])

    @pl.when(is_home)
    def _():
        for q in range(3):
            home_copy(q).start()

    def stage_copy(q):
        return pltpu.make_async_copy(src[q], stage.at[q], staged.at[q])

    @pl.when(jnp.logical_not(is_home))
    def _():
        for q in range(3):
            stage_copy(q).start()

    v = tok_ref[...].astype(jnp.float32)
    ms = jnp.mean(v * v, axis=-1, keepdims=True)
    xz[g] = (v * lax.rsqrt(ms + EPSILON) * gain_ref[...]).astype(jnp.bfloat16)
    for q in range(3):
        W[q][CAP] = jnp.zeros((BS, BS), jnp.bfloat16)

    tabs[2] = tab_ref[...]
    pl.semaphore_wait(barrier, len(peers))

    gcopies = [remote(xz.at[g], xz.at[g], gs.at[i], gr.at[i], gpeer[i]) for i in (1, 2, 3)]
    pending.extend(gcopies)

    @pl.when(jnp.logical_not(is_home))
    def _():
        for q in range(3):
            stage_copy(q).wait()
            swap_copy(q).start()

    tcopy = remote(tab_ref, tabs.at[c], ssem.at[0], tsem.at[0], sib)
    tcopy.start()

    def core_send(q, ref):
        remote(ref, ref, cs.at[q], cr.at[q], sib).start()

    def x_copy(q, k, m):
        ref = piece(q, m, x)
        return remote(ref, ref, xs.at[q, k, m], xr.at[q, k, m], left if k else right)

    def f_copy(q, m):
        ref, p = (piece(q, m, x + 1), left) if m % 2 else (piece(q, m, x + 3), right)
        return remote(ref, ref, fs.at[q, m], fr.at[q, m], p)

    def x_send(q, m):
        x_copy(q, 0, m).start()
        x_copy(q, 1, m).start()

    def step(q, m):
        ref = piece(q, m, x)
        remote(ref, ref, zs.at[q, 0, m], zr.at[q, key[m]], above).wait_recv()

        @pl.when(goes_up[m])
        def _():
            z_up(q, m).start()

        @pl.when(goes_down[m])
        def _():
            z_down(q, m).start()

        x_send(q, m)
        core_send(q, ref)

    def forward(q, m):
        fl, fright = piece(q, m, x + 3), piece(q, m, x + 1)
        remote(fl, fl, xs.at[q, 0, m], xr.at[q, 0, m], right).wait_recv()
        remote(fright, fright, xs.at[q, 1, m], xr.at[q, 1, m], left).wait_recv()
        f_copy(q, m).start()
        core_send(q, fl)
        core_send(q, fright)

    def far(q, m):
        ref = piece(q, m, x + 2)
        remote(ref, ref, fs.at[q, m], fr.at[q, m], right).wait_recv()
        core_send(q, ref)

    def stage4(q):
        ref = W[q].at[pl.ds(48 * (1 - c), 48)]
        remote(ref, ref, cs.at[q], cr.at[q], sib).wait_recv()

    def w4(q, j, k):
        def one(jj, kk):
            b = jj * 32 + kk
            return W[q][tab_s[2 * q + b // 128, b % 128]]
        return one(j, k), one(j, k + 1), one(j + 1, k), one(j + 1, k + 1)

    def project(q, jp):
        acc = jnp.zeros((64, 256), jnp.float32)
        for kk in range(16):
            a, b, e, f = w4(q, 2 * jp, 2 * kk)
            w = jnp.concatenate(
                [jnp.concatenate([a, e], axis=1), jnp.concatenate([b, f], axis=1)], axis=0)
            xx = xa[:, :, 256 * kk:256 * kk + 256].reshape(64, 256)
            acc = acc + jnp.dot(xx, w, preferred_element_type=jnp.float32)
        return acc

    def tokens_g():
        for i in (1, 2, 3):
            ref = xz.at[(g + 4 - i) % 4]
            remote(ref, ref, gs.at[i], gr.at[i], gpeer[i]).wait_recv()
        for i in range(4):
            xf[4 * i:4 * i + 4, :] = xz[i].astype(jnp.float32)
        xa[y] = xf[...].astype(jnp.bfloat16)
        for i in (1, 2, 3):
            cp = remote(xa.at[y], xa.at[y], ys.at[i], yr.at[i], ypeer[i])
            cp.start()
            pending.append(cp)

    def tokens_y():
        for i in (1, 2, 3):
            ref = xa.at[(y + 4 - i) % 4]
            remote(ref, ref, ys.at[i], yr.at[i], ypeer[i]).wait_recv()
        remote(tab_ref, tabs.at[1 - c], ssem.at[0], tsem.at[0], sib).wait_recv()
        mine = pltpu.make_async_copy(tabs.at[jnp.where(is_home, 2, half)], tab_s, tsem.at[1])
        mine.start()
        mine.wait()

    items = [(q, m) for q in range(3) for m in range(4)]

    @pl.when(is_home)
    def _():
        for q in range(3):
            step(q, 0)

    def other_step(p):
        @pl.when(jnp.logical_not(is_home))
        def _():
            step(*items[p])

    other_step(0)
    step(*items[1])
    step(*items[2])
    step(*items[3])
    other_step(4)
    forward(*items[0])
    step(*items[5])
    forward(*items[1])
    step(*items[6])
    forward(*items[2])
    for cp in gcopies:
        cp.start()
    step(*items[7])
    forward(*items[3])
    other_step(8)
    forward(*items[4])
    far(*items[0])
    step(*items[9])
    forward(*items[5])
    far(*items[1])
    step(*items[10])
    forward(*items[6])
    far(*items[2])
    step(*items[11])
    forward(*items[7])
    far(*items[3])
    forward(*items[8])
    far(*items[4])
    tokens_g()
    forward(*items[9])
    far(*items[5])
    forward(*items[10])
    far(*items[6])
    tokens_y()
    forward(*items[11])
    stage4(0)
    for jp in range(4):
        gate_s[jp] = project(0, jp)
    far(*items[7])
    stage4(1)
    for jp in range(4):
        up = project(1, jp)
        ga = gate_s[jp]
        hid_s[jp] = (ga / (1.0 + jnp.exp(-ga)) * up).astype(jnp.bfloat16)
    far(*items[8])
    far(*items[9])
    far(*items[10])
    far(*items[11])
    stage4(2)

    def y_copy(n, i):
        return remote(sb.at[n, (y + i) % 4], rb.at[n, i], ys2.at[n, i], yr2.at[n, i], ypeer[i])

    def g_copy(n, i):
        return remote(gb.at[n, (g + i) % 4], rg.at[n, i], gs2.at[n, i], gr2.at[n, i], gpeer[i])

    for n in range(CH):
        for kp in range(4):
            acc = jnp.zeros((64, 256), jnp.float32)
            for jp in range(4):
                k = n * 8 + 2 * kp
                a, e, b, f = w4(2, 2 * jp, k)
                w = jnp.concatenate(
                    [jnp.concatenate([a, e], axis=1), jnp.concatenate([b, f], axis=1)], axis=0)
                acc = acc + jnp.dot(hid_s[jp], w, preferred_element_type=jnp.float32)
            sb[n, :, :, 256 * kp:256 * kp + 256] = acc.astype(jnp.bfloat16).reshape(4, 16, 256)
        for i in (1, 2, 3):
            y_copy(n, i).start()

    for n in range(CH):
        for i in (1, 2, 3):
            y_copy(n, i).wait_recv()
        s = sb[n, y].astype(jnp.float32)
        for i in (1, 2, 3):
            s = s + rb[n, i].astype(jnp.float32)
        sf[...] = s
        for i in range(4):
            gb[n, i] = sf[4 * i:4 * i + 4, :].astype(jnp.bfloat16)
        for i in (1, 2, 3):
            g_copy(n, i).start()

    for n in range(CH):
        for i in (1, 2, 3):
            g_copy(n, i).wait_recv()
        s = gb[n, g].astype(jnp.float32)
        for i in (1, 2, 3):
            s = s + rg[n, i].astype(jnp.float32)
        cols = slice(n * CW, (n + 1) * CW)
        out_ref[:, cols] = (tok_ref[:, cols].astype(jnp.float32) + s).astype(jnp.bfloat16)

    for cp in pending:
        cp.wait_send()
    tcopy.wait_send()
    for q in range(3):
        for m in range(4):
            x_copy(q, 0, m).wait_send()
            x_copy(q, 1, m).wait_send()
            f_copy(q, m).wait_send()
        for m in range(4):
            @pl.when(goes_up[m])
            def _():
                z_up(q, m).wait_send()

            @pl.when(goes_down[m])
            def _():
                z_down(q, m).wait_send()

    for q in range(3):
        ref = W[q].at[pl.ds(48 * c, 48)]
        remote(ref, ref, cs.at[q], cr.at[q], sib).wait_send()
    for n in range(CH):
        for i in (1, 2, 3):
            y_copy(n, i).wait_send()
            g_copy(n, i).wait_send()

    @pl.when(jnp.logical_not(is_home))
    def _():
        for q in range(3):
            swap_copy(q).wait_send()


def shards(tokens, norm_gain, gate_slots, up_slots, down_slots, gate_ids, up_ids, down_ids):
    ids = jnp.stack([gate_ids, up_ids, down_ids])
    hit = ids[:, None, :] == jnp.arange(256, dtype=jnp.int32)[None, :, None]
    tab = jnp.min(jnp.where(hit, jnp.arange(CAP, dtype=jnp.int32), CAP), axis=-1)
    tab = jnp.pad(tab.reshape(6, 128), ((0, 2), (0, 0)))
    bf, f32 = jnp.bfloat16, jnp.float32
    dma = pltpu.SemaphoreType.DMA
    vm = pl.BlockSpec(memory_space=pltpu.VMEM)
    hbm = pl.BlockSpec(memory_space=pltpu.MemorySpace.HBM)
    return pl.pallas_call(
        layer,
        out_shape=jax.ShapeDtypeStruct((4, D), bf),
        in_specs=[vm, vm, vm, hbm, hbm, hbm],
        out_specs=vm,
        scratch_shapes=[
            pltpu.VMEM((CAP + 1, BS, BS), bf),
            pltpu.VMEM((CAP + 1, BS, BS), bf),
            pltpu.VMEM((CAP + 1, BS, BS), bf),
            pltpu.VMEM((3, 8, 128), jnp.int32),
            pltpu.SMEM((8, 128), jnp.int32),
            pltpu.VMEM((4, 4, D), bf),
            pltpu.VMEM((16, D), f32),
            pltpu.VMEM((4, 16, D), bf),
            pltpu.VMEM((4, 64, 256), f32),
            pltpu.VMEM((4, 64, 256), bf),
            pltpu.VMEM((CH, 4, 16, CW), bf),
            pltpu.VMEM((CH, 4, 16, CW), bf),
            pltpu.VMEM((16, CW), f32),
            pltpu.VMEM((CH, 4, 4, CW), bf),
            pltpu.VMEM((CH, 4, 4, CW), bf),
            pltpu.VMEM((3, 3, BS, BS), bf),
            dma((3,)), dma((3,)), dma((3, 4)), dma((3, 2, 4)), dma((3, 2, 4)), dma((3, 2, 4)),
            dma((3, 4)), dma((3, 4)), dma((3,)), dma((3,)), dma((2,)), dma((1,)),
            dma((4,)), dma((4,)), dma((4,)), dma((4,)),
            dma((CH, 4)), dma((CH, 4)), dma((CH, 4)), dma((CH, 4)),
        ],
        compiler_params=pltpu.CompilerParams(
            collective_id=0, has_side_effects=True, vmem_limit_bytes=63 << 20),
    )(tokens, norm_gain.reshape(1, D), tab, gate_slots, up_slots, down_slots)


def solution(mesh):
    placed = (
        P(("tp", "dp"), None),
        P(),
        P(("tp", "dp"), None, None),
        P(("tp", "dp"), None, None),
        P(("tp", "dp"), None, None),
        P("tp"),
        P("tp"),
        P("tp"),
    )
    return jax.shard_map(
        shards, mesh=mesh, in_specs=placed, out_specs=P(("tp", "dp"), None), check_vma=False
    )
```

```python
import jax
import jax.numpy as jnp
from jax import lax
from jax.experimental import pallas as pl
from jax.experimental.pallas import tpu as pltpu
from jax.sharding import PartitionSpec as P

EPSILON = 1e-05
MESH = pl.DeviceIdType.MESH
BS = 128
CAP = 96
D = 4096
CH = 4
CW = D // CH


def layer(tok_ref, gain_ref, tab_ref, g_hbm, u_hbm, d_hbm, out_ref,
          wg, wu, wd, tabs, tab_s, xz, xf, xa, gate_s, hid_s, sb, rb, sf, gb, rg, stage,
          swap, staged, zr, zs, xr, xs, fr, fs, cr, cs, tsem, ssem, gr, gs, yr, ys, yr2, ys2, gr2, gs2):
    t = lax.axis_index("tp")
    d = lax.axis_index("dp")
    hi, y, c = t // 8, (t // 2) % 4, t % 2
    zl, x = d // 4, d % 4
    half, ze = zl // 4, zl % 4
    g = hi * 2 + half

    def dev(hi=hi, y=y, c=c, half=half, ze=ze, x=x):
        return {"tp": hi * 8 + y * 2 + c, "dp": (half * 4 + ze) * 4 + x}

    entry = dev(c=1 - c, half=1 - half, ze=3 * half)
    across = [dev(c=1 - c, half=1 - half, ze=i) for i in range(4)]
    right, left = dev(x=(x + 1) % 4), dev(x=(x + 3) % 4)
    sib = dev(c=1 - c)
    ypeer = [None] + [dev(y=(y + i) % 4) for i in (1, 2, 3)]
    gpeer = [None]
    for i in (1, 2, 3):
        o = (g + i) % 4
        gpeer.append(dev(hi=o // 2, half=o % 2))

    barrier = pltpu.get_barrier_semaphore()
    peers = across + [right, left, sib] + ypeer[1:] + gpeer[1:] + [
        dev(ze=(ze + 1) % 4), dev(ze=(ze + 3) % 4)]
    for p in peers:
        pl.semaphore_signal(barrier, inc=1, device_id=p, device_id_type=MESH)
    W = (wg, wu, wd)
    src = (g_hbm, u_hbm, d_hbm)
    is_home = c == half
    pending = []

    def remote(a, b, s, r, p):
        return pltpu.make_async_remote_copy(
            src_ref=a, dst_ref=b, send_sem=s, recv_sem=r, device_id=p, device_id_type=MESH)

    edge = (ze == 0) | (ze == 3)
    order = (0, jnp.where(ze == 0, 3, 1), jnp.where(edge, 2, 3),
             jnp.where(ze == 0, 1, jnp.where(ze == 3, 3, 2)))
    zpos = [jnp.where(is_home, (ze + 4 - order[m]) % 4, jnp.where(half == 0, m, 3 - m)) for m in range(4)]
    key = [jnp.where(is_home, order[m], m) for m in range(4)]
    goes_up = [(ze < 3) & jnp.where(is_home, ze >= order[m], half == 1) for m in range(4)]
    goes_down = [(ze > 0) & jnp.where(is_home, (ze < order[m]) | (m == 0), half == 0) for m in range(4)]
    above = dev(ze=jnp.minimum(ze + 1, 3))
    below = dev(ze=jnp.maximum(ze - 1, 0))

    def piece(q, m, xx):
        return W[q].at[pl.ds((16 * c + 4 * zpos[m] + xx % 4) * 3, 3)]

    def z_up(q, m):
        ref = piece(q, m, x)
        return remote(ref, ref, zs.at[q, 0, m], zr.at[q, jnp.where(is_home, (order[m] + 1) % 4, m)], above)

    def z_down(q, m):
        ref = piece(q, m, x)
        return remote(ref, ref, zs.at[q, 1, m], zr.at[q, jnp.where(is_home, (order[m] + 3) % 4, m)], below)

    def swap_copy(q):
        p = 16 * half + 4 * ze + x
        m = jnp.where(half == 1, ze, 3 - ze)
        return remote(stage.at[q], W[q].at[pl.ds(p * 3, 3)], swap.at[q], zr.at[q, m], entry)

    def home_copy(q):
        return pltpu.make_async_copy(src[q], piece(q, 0, x), zr.at[q, 0])

    @pl.when(is_home)
    def _():
        for q in range(3):
            home_copy(q).start()

    def stage_copy(q):
        return pltpu.make_async_copy(src[q], stage.at[q], staged.at[q])

    @pl.when(jnp.logical_not(is_home))
    def _():
        for q in range(3):
            stage_copy(q).start()

    v = tok_ref[...].astype(jnp.float32)
    ms = jnp.mean(v * v, axis=-1, keepdims=True)
    xz[g] = (v * lax.rsqrt(ms + EPSILON) * gain_ref[...]).astype(jnp.bfloat16)
    for q in range(3):
        W[q][CAP] = jnp.zeros((BS, BS), jnp.bfloat16)

    tabs[2] = tab_ref[...]
    pl.semaphore_wait(barrier, len(peers))

    gcopies = [remote(xz.at[g], xz.at[g], gs.at[i], gr.at[i], gpeer[i]) for i in (1, 2, 3)]
    pending.extend(gcopies)

    @pl.when(jnp.logical_not(is_home))
    def _():
        for q in range(3):
            stage_copy(q).wait()
        for q in range(1):
            swap_copy(q).start()

    tcopy = remote(tab_ref, tabs.at[c], ssem.at[0], tsem.at[0], sib)
    tcopy.start()

    def core_send(q, ref):
        remote(ref, ref, cs.at[q], cr.at[q], sib).start()

    def x_copy(q, k, m):
        ref = piece(q, m, x)
        return remote(ref, ref, xs.at[q, k, m], xr.at[q, k, m], left if k else right)

    def f_copy(q, m):
        ref, p = (piece(q, m, x + 1), left) if m % 2 else (piece(q, m, x + 3), right)
        return remote(ref, ref, fs.at[q, m], fr.at[q, m], p)

    def x_send(q, m):
        x_copy(q, 0, m).start()
        x_copy(q, 1, m).start()

    def step(q, m):
        ref = piece(q, m, x)
        remote(ref, ref, zs.at[q, 0, m], zr.at[q, key[m]], above).wait_recv()

        @pl.when(goes_up[m])
        def _():
            z_up(q, m).start()

        @pl.when(goes_down[m])
        def _():
            z_down(q, m).start()

        x_send(q, m)
        core_send(q, ref)

    def forward(q, m):
        fl, fright = piece(q, m, x + 3), piece(q, m, x + 1)
        remote(fl, fl, xs.at[q, 0, m], xr.at[q, 0, m], right).wait_recv()
        remote(fright, fright, xs.at[q, 1, m], xr.at[q, 1, m], left).wait_recv()
        f_copy(q, m).start()
        core_send(q, fl)
        core_send(q, fright)

    def far(q, m):
        ref = piece(q, m, x + 2)
        remote(ref, ref, fs.at[q, m], fr.at[q, m], right).wait_recv()
        core_send(q, ref)

    def stage4(q):
        ref = W[q].at[pl.ds(48 * (1 - c), 48)]
        remote(ref, ref, cs.at[q], cr.at[q], sib).wait_recv()

    def w4(q, j, k):
        def one(jj, kk):
            b = jj * 32 + kk
            return W[q][tab_s[2 * q + b // 128, b % 128]]
        return one(j, k), one(j, k + 1), one(j + 1, k), one(j + 1, k + 1)

    def project(q, jp):
        acc = jnp.zeros((64, 256), jnp.float32)
        for kk in range(16):
            a, b, e, f = w4(q, 2 * jp, 2 * kk)
            w = jnp.concatenate(
                [jnp.concatenate([a, e], axis=1), jnp.concatenate([b, f], axis=1)], axis=0)
            xx = xa[:, :, 256 * kk:256 * kk + 256].reshape(64, 256)
            acc = acc + jnp.dot(xx, w, preferred_element_type=jnp.float32)
        return acc

    def tokens_g():
        for i in (1, 2, 3):
            ref = xz.at[(g + 4 - i) % 4]
            remote(ref, ref, gs.at[i], gr.at[i], gpeer[i]).wait_recv()
        for i in range(4):
            xf[4 * i:4 * i + 4, :] = xz[i].astype(jnp.float32)
        xa[y] = xf[...].astype(jnp.bfloat16)
        for i in (1, 2, 3):
            cp = remote(xa.at[y], xa.at[y], ys.at[i], yr.at[i], ypeer[i])
            cp.start()
            pending.append(cp)

    def tokens_y():
        for i in (1, 2, 3):
            ref = xa.at[(y + 4 - i) % 4]
            remote(ref, ref, ys.at[i], yr.at[i], ypeer[i]).wait_recv()
        remote(tab_ref, tabs.at[1 - c], ssem.at[0], tsem.at[0], sib).wait_recv()
        mine = pltpu.make_async_copy(tabs.at[jnp.where(is_home, 2, half)], tab_s, tsem.at[1])
        mine.start()
        mine.wait()

    items = [(q, m) for q in range(3) for m in range(4)]

    @pl.when(is_home)
    def _():
        for q in range(3):
            step(q, 0)

    def later_swap(q):
        @pl.when(jnp.logical_not(is_home))
        def _():
            swap_copy(q).start()

    def later_home(q):
        @pl.when(is_home)
        def _():
            step(q, 0)

    def other_step(p):
        @pl.when(jnp.logical_not(is_home))
        def _():
            step(*items[p])

    other_step(0)
    later_swap(1)
    step(*items[1])
    step(*items[2])
    later_swap(2)
    step(*items[3])
    other_step(4)
    forward(*items[0])
    step(*items[5])
    forward(*items[1])
    step(*items[6])
    forward(*items[2])
    for cp in gcopies:
        cp.start()
    step(*items[7])
    forward(*items[3])
    other_step(8)
    forward(*items[4])
    far(*items[0])
    step(*items[9])
    forward(*items[5])
    far(*items[1])
    step(*items[10])
    forward(*items[6])
    far(*items[2])
    step(*items[11])
    forward(*items[7])
    far(*items[3])
    forward(*items[8])
    far(*items[4])
    tokens_g()
    forward(*items[9])
    far(*items[5])
    forward(*items[10])
    far(*items[6])
    tokens_y()
    forward(*items[11])
    stage4(0)
    for jp in range(4):
        gate_s[jp] = project(0, jp)
    far(*items[7])
    stage4(1)
    for jp in range(4):
        up = project(1, jp)
        ga = gate_s[jp]
        hid_s[jp] = (ga / (1.0 + jnp.exp(-ga)) * up).astype(jnp.bfloat16)
    far(*items[8])
    far(*items[9])
    far(*items[10])
    far(*items[11])
    stage4(2)

    def y_copy(n, i):
        return remote(sb.at[n, (y + i) % 4], rb.at[n, i], ys2.at[n, i], yr2.at[n, i], ypeer[i])

    def g_copy(n, i):
        return remote(gb.at[n, (g + i) % 4], rg.at[n, i], gs2.at[n, i], gr2.at[n, i], gpeer[i])

    for n in range(CH):
        for kp in range(4):
            acc = jnp.zeros((64, 256), jnp.float32)
            for jp in range(4):
                k = n * 8 + 2 * kp
                a, e, b, f = w4(2, 2 * jp, k)
                w = jnp.concatenate(
                    [jnp.concatenate([a, e], axis=1), jnp.concatenate([b, f], axis=1)], axis=0)
                acc = acc + jnp.dot(hid_s[jp], w, preferred_element_type=jnp.float32)
            sb[n, :, :, 256 * kp:256 * kp + 256] = acc.astype(jnp.bfloat16).reshape(4, 16, 256)
        for i in (1, 2, 3):
            y_copy(n, i).start()

    for n in range(CH):
        for i in (1, 2, 3):
            y_copy(n, i).wait_recv()
        s = sb[n, y].astype(jnp.float32)
        for i in (1, 2, 3):
            s = s + rb[n, i].astype(jnp.float32)
        sf[...] = s
        for i in range(4):
            gb[n, i] = sf[4 * i:4 * i + 4, :].astype(jnp.bfloat16)
        for i in (1, 2, 3):
            g_copy(n, i).start()

    for n in range(CH):
        for i in (1, 2, 3):
            g_copy(n, i).wait_recv()
        s = gb[n, g].astype(jnp.float32)
        for i in (1, 2, 3):
            s = s + rg[n, i].astype(jnp.float32)
        cols = slice(n * CW, (n + 1) * CW)
        out_ref[:, cols] = (tok_ref[:, cols].astype(jnp.float32) + s).astype(jnp.bfloat16)

    for cp in pending:
        cp.wait_send()
    tcopy.wait_send()
    for q in range(3):
        for m in range(4):
            x_copy(q, 0, m).wait_send()
            x_copy(q, 1, m).wait_send()
            f_copy(q, m).wait_send()
        for m in range(4):
            @pl.when(goes_up[m])
            def _():
                z_up(q, m).wait_send()

            @pl.when(goes_down[m])
            def _():
                z_down(q, m).wait_send()

    for q in range(3):
        ref = W[q].at[pl.ds(48 * c, 48)]
        remote(ref, ref, cs.at[q], cr.at[q], sib).wait_send()
    for n in range(CH):
        for i in (1, 2, 3):
            y_copy(n, i).wait_send()
            g_copy(n, i).wait_send()

    @pl.when(jnp.logical_not(is_home))
    def _():
        for q in range(3):
            swap_copy(q).wait_send()


def shards(tokens, norm_gain, gate_slots, up_slots, down_slots, gate_ids, up_ids, down_ids):
    ids = jnp.stack([gate_ids, up_ids, down_ids])
    hit = ids[:, None, :] == jnp.arange(256, dtype=jnp.int32)[None, :, None]
    tab = jnp.min(jnp.where(hit, jnp.arange(CAP, dtype=jnp.int32), CAP), axis=-1)
    tab = jnp.pad(tab.reshape(6, 128), ((0, 2), (0, 0)))
    bf, f32 = jnp.bfloat16, jnp.float32
    dma = pltpu.SemaphoreType.DMA
    vm = pl.BlockSpec(memory_space=pltpu.VMEM)
    hbm = pl.BlockSpec(memory_space=pltpu.MemorySpace.HBM)
    return pl.pallas_call(
        layer,
        out_shape=jax.ShapeDtypeStruct((4, D), bf),
        in_specs=[vm, vm, vm, hbm, hbm, hbm],
        out_specs=vm,
        scratch_shapes=[
            pltpu.VMEM((CAP + 1, BS, BS), bf),
            pltpu.VMEM((CAP + 1, BS, BS), bf),
            pltpu.VMEM((CAP + 1, BS, BS), bf),
            pltpu.VMEM((3, 8, 128), jnp.int32),
            pltpu.SMEM((8, 128), jnp.int32),
            pltpu.VMEM((4, 4, D), bf),
            pltpu.VMEM((16, D), f32),
            pltpu.VMEM((4, 16, D), bf),
            pltpu.VMEM((4, 64, 256), f32),
            pltpu.VMEM((4, 64, 256), bf),
            pltpu.VMEM((CH, 4, 16, CW), bf),
            pltpu.VMEM((CH, 4, 16, CW), bf),
            pltpu.VMEM((16, CW), f32),
            pltpu.VMEM((CH, 4, 4, CW), bf),
            pltpu.VMEM((CH, 4, 4, CW), bf),
            pltpu.VMEM((3, 3, BS, BS), bf),
            dma((3,)), dma((3,)), dma((3, 4)), dma((3, 2, 4)), dma((3, 2, 4)), dma((3, 2, 4)),
            dma((3, 4)), dma((3, 4)), dma((3,)), dma((3,)), dma((2,)), dma((1,)),
            dma((4,)), dma((4,)), dma((4,)), dma((4,)),
            dma((CH, 4)), dma((CH, 4)), dma((CH, 4)), dma((CH, 4)),
        ],
        compiler_params=pltpu.CompilerParams(
            collective_id=0, has_side_effects=True, vmem_limit_bytes=63 << 20),
    )(tokens, norm_gain.reshape(1, D), tab, gate_slots, up_slots, down_slots)


def solution(mesh):
    placed = (
        P(("tp", "dp"), None),
        P(),
        P(("tp", "dp"), None, None),
        P(("tp", "dp"), None, None),
        P(("tp", "dp"), None, None),
        P("tp"),
        P("tp"),
        P("tp"),
    )
    return jax.shard_map(
        shards, mesh=mesh, in_specs=placed, out_specs=P(("tp", "dp"), None), check_vma=False
    )
```
